32 devices in a mesh: polar: 4 (over y, x), azimuth: 8 (over z, core).
Axes of the slice: x: 2, y: 2, z: 4, core: 2. Of those that a mesh axis runs over, the one named last changes fastest.
Arguments:
- grid_state: bfloat16 [32, 512, 640], P('polar', 'azimuth'), may hold values from -6 to 6
- filter_taps: bfloat16 [32, 9, 4, 129], P('polar'), may hold values from -0.59765625 to 0.59765625
- support_start: int32 [32], P('polar'), may hold values from -64 to 64, as said below
- support_count: int32 [32], P('polar'), may hold values from 1 to 129
- filter_mix: bfloat16 [2, 9, 640], replicated, may hold values from -2 to 2
- w_in: bfloat16 [2, 640, 1280], replicated, may hold values from -0.25 to 0.25
- w_out: bfloat16 [2, 1280, 640], replicated, may hold values from -0.15625 to 0.15625
Outputs:
- next_state: bfloat16 [32, 512, 640], P('polar', 'azimuth')
The draws below stay inside these ranges and needn't reach their ends.
Inputs may be any that keep to these rules, and one draw needn't show every extreme that they name: support_start[i] + support_count[i] - 1 <= 64; support is widest near the poles.
All inputs are finite; a program needn't handle non-finite values.
Results may differ from the reference program's by a relative error of at most 0.006.
Values may be sent and summed in bfloat16 or wider, within the bound.
No kernel may reach another device: no remote copies, remote signals or barrier semaphores. Data moves between devices by JAX's collectives and lax.ppermute only.
A program may use at most 64 MiB of HBM per device.

```python
import jax
import jax.numpy as jnp
from jax import lax

C = 640
HID = 1280
FILTERS = 9
ROWS = 4
LAYERS = 2
LON_DEV = 64
HALF = 64
TAPS = 129
NLAT = 32
NLON = 512


def support_tables(key):
    latitude = jnp.arange(NLAT, dtype=jnp.int32)
    polar_gap = jnp.minimum(latitude, NLAT - 1 - latitude)
    widest = TAPS // (polar_gap + 1)
    jitter = jax.random.randint(jax.random.fold_in(key, 11), (NLAT,), 0, 9, dtype=jnp.int32)
    counts = jnp.clip(widest + jitter, 1, TAPS)
    middle = latitude == NLAT // 2
    counts = jnp.where(middle, 1, counts)
    slack = TAPS - counts
    raw_shift = jax.random.randint(jax.random.fold_in(key, 12), (NLAT,), 0, 1048576, dtype=jnp.int32)
    starts = raw_shift % (slack + 1) - HALF
    starts = jnp.where(middle, HALF, starts)
    return (starts.astype(jnp.int32), counts.astype(jnp.int32))


def draw_support_start(key, part):
    return support_tables(key)[0]


def draw_support_count(key, part):
    return support_tables(key)[1]


def level_of(key, dims, pieces, smallest, largest):
    def one(dim, shards_of):
        steps = jax.random.uniform(jax.random.fold_in(jax.random.fold_in(key, 6), dim), (shards_of,), jnp.float32, smallest / len(pieces), largest / len(pieces))
        return jnp.repeat(jnp.exp(steps), dims[dim] // shards_of).reshape((-1,) + (1,) * (len(dims) - dim - 1))

    level = one(*pieces[0])
    for cut in pieces[1:]:
        level = level * one(*cut)
    return level


def bell_draw(rng, extent, scale, limit, pieces=(), kind=jnp.bfloat16):
    gain = level_of(rng, extent, pieces, -0.22, 0.18) if pieces else 1.0
    entries = jax.random.normal(rng, extent, jnp.float32) * scale * gain
    return jnp.minimum(jnp.maximum(entries, -limit), limit).astype(kind)


def setup_inputs(seed: int = 0) -> dict:
    arg_keys = jax.random.split(jax.random.key(seed), 8)
    grid_state = bell_draw(arg_keys[0], (NLAT, NLON, C), 1.0, 6.0, ((0, 4), (1, 8)))
    filter_taps = bell_draw(arg_keys[1], (NLAT, FILTERS, ROWS, TAPS), 0.1, 0.59765625, ((0, 4),))
    support_start = draw_support_start(jax.random.fold_in(arg_keys[7], 71), 0)
    support_count = draw_support_count(jax.random.fold_in(arg_keys[7], 71), 0)
    filter_mix = bell_draw(arg_keys[4], (LAYERS, FILTERS, C), 0.35, 2.0)
    w_in = bell_draw(arg_keys[5], (LAYERS, C, HID), C ** -0.5, 0.25)
    w_out = bell_draw(arg_keys[6], (LAYERS, HID, C), HID ** -0.5, 0.15625)
    return dict(grid_state=grid_state, filter_taps=filter_taps, support_start=support_start, support_count=support_count, filter_mix=filter_mix, w_in=w_in, w_out=w_out)


def tap_bands(filter_taps, support_start, support_count, reach):
    tap_count = filter_taps.shape[-1]
    offsets = jnp.arange(tap_count, dtype=jnp.int32) - reach
    inside = (offsets[None, :] >= support_start[:, None]) & (offsets[None, :] < (support_start + support_count)[:, None])
    masked = jnp.where(inside[:, None, None, :], filter_taps.astype(jnp.float32), jnp.float32(0.0))
    column = jnp.arange(reach, dtype=jnp.int32)[:, None]
    window = jnp.arange(3 * reach, dtype=jnp.int32)[None, :]
    onehot = ((window - column)[:, :, None] == jnp.arange(tap_count, dtype=jnp.int32)[None, None, :]).astype(jnp.float32)
    return jnp.einsum("akrt,jwt->akjrw", masked, onehot).astype(jnp.bfloat16)


def block_windows(rows, reach):
    blocks = rows.shape[1] // reach
    extended = jnp.concatenate([rows[:, -reach:], rows, rows[:, :reach]], axis=1)
    extended = extended.reshape(rows.shape[0], blocks + 2, reach, rows.shape[2])
    return jnp.concatenate([extended[:, :blocks], extended[:, 1:blocks + 1], extended[:, 2:]], axis=2)


def channel_mlp(act, field, first, second):
    flat = act.reshape(-1, act.shape[-1])
    hidden = jax.nn.gelu(jnp.dot(flat, first, preferred_element_type=jnp.float32), approximate=False).astype(jnp.bfloat16)
    update = jnp.dot(hidden, second, preferred_element_type=jnp.float32)
    return (field.astype(jnp.float32) + update.reshape(field.shape)).astype(jnp.bfloat16)


def reference(grid_state, filter_taps, support_start, support_count, filter_mix, w_in, w_out):
    bands = tap_bands(filter_taps, support_start, support_count, LON_DEV)
    field = grid_state
    for layer_no in range(LAYERS):
        padded = jnp.pad(field, ((2, 1), (0, 0), (0, 0)))
        mix_row = filter_mix[layer_no].astype(jnp.float32)

        def one_latitude(lat_index):
            rows = lax.dynamic_slice_in_dim(padded, lat_index, 4, 0)
            windows = block_windows(rows, LON_DEV).astype(jnp.float32)
            band_rows = lax.dynamic_index_in_dim(bands, lat_index, 0, keepdims=False).astype(jnp.float32)
            conv = jnp.einsum("kjrw,rbwc->kbjc", band_rows, windows)
            mixed = jnp.einsum("kbjc,kc->bjc", conv, mix_row)
            return jax.nn.gelu(mixed, approximate=False).astype(jnp.bfloat16).reshape(NLON, C)

        act = lax.map(one_latitude, jnp.arange(NLAT, dtype=jnp.int32))
        field = channel_mlp(act, field, w_in[layer_no], w_out[layer_no])
    return field
```

```python
import functools

import jax
import jax.numpy as jnp
from jax import lax
from jax.experimental import pallas as pl
from jax.experimental.pallas import tpu as pltpu
from jax.sharding import PartitionSpec as P

F32 = jnp.float32
BF16 = jnp.bfloat16
ROWS = 4
STRIP = 16


def hbm():
    return pl.BlockSpec(memory_space=pl.ANY)


def pinned():
    return pl.BlockSpec(memory_space=pltpu.HBM)


def vmem():
    return pl.BlockSpec(memory_space=pltpu.VMEM)


def smem():
    return pl.BlockSpec(memory_space=pltpu.SMEM)


def gelu(x):
    return 0.5 * x * (1.0 + lax.erf(x * 0.7071067811865476))


def masked_rows(filter_taps, support_start, support_count, reach):
    lats, filters, rows, taps = filter_taps.shape
    wide = 4 * reach
    offset = jnp.arange(wide, dtype=jnp.int32) - reach
    inside = (offset[None] >= support_start[:, None]) & (
        offset[None] < (support_start + support_count)[:, None]
    )
    flat = filter_taps.reshape(lats, filters * rows, taps)
    flat = jnp.pad(flat, ((0, 0), (0, 0), (0, wide - taps))).astype(F32)
    return jnp.where(inside[:, None, :], flat, 0.0)


def shift_table(reach):
    wide, strips = 4 * reach, reach // STRIP
    column = jnp.arange(3 * strips * 2 * reach, dtype=jnp.int32)
    section, strip = column // (strips * 2 * reach), column // (2 * reach) % strips
    lane = column % (2 * reach)
    tap = (section * reach - STRIP * strip + lane % reach) % wide
    source = lane // reach * wide + tap
    return (jnp.arange(2 * wide, dtype=jnp.int32)[:, None] == source[None, :]).astype(BF16)


def band_kernel(filters, reach, parity, taps, table, band_out, base, band, sem):
    lats = taps.shape[0]
    wide, strips = 4 * reach, reach // STRIP
    order = [2 - parity[0], 0, 1 + parity[0]]

    def flush(a):
        return pltpu.make_async_copy(band.at[a], band_out.at[a], sem.at[a])

    def one(a, carry):
        for k in range(filters):
            for r in range(ROWS):
                row = taps[a, k * ROWS + r : k * ROWS + r + 1, :]
                skew = pltpu.roll(
                    jnp.broadcast_to(row, (STRIP, wide)), 0, 1, stride=1, stride_axis=0
                )
                base[r // 2, k * STRIP : (k + 1) * STRIP, r % 2 * wide : (r % 2 + 1) * wide] = (
                    skew.astype(BF16)
                )
        span = strips * 2 * reach
        for pair in range(ROWS // 2):
            for s in range(3):
                rolled = jnp.dot(
                    base[pair], table[:, s * span : (s + 1) * span], preferred_element_type=F32
                ).astype(BF16)
                for k in range(filters):
                    for b in range(strips):
                        row = k * reach + STRIP * b
                        band[
                            a,
                            order[s],
                            row : row + STRIP,
                            pair * 2 * reach : (pair + 1) * 2 * reach,
                        ] = rolled[k * STRIP : (k + 1) * STRIP, b * 2 * reach : (b + 1) * 2 * reach]
        flush(a).start()
        return carry

    lax.fori_loop(0, lats, one, 0)
    for a in range(lats):
        flush(a).wait()


def make_bands(taps, parity, filters, reach):
    lats = taps.shape[0]
    shape = (lats, 3, filters * reach, ROWS * reach)
    return pl.pallas_call(
        functools.partial(band_kernel, filters, reach),
        out_shape=jax.ShapeDtypeStruct(shape, BF16),
        in_specs=[smem(), vmem(), vmem()],
        out_specs=pinned(),
        scratch_shapes=[
            pltpu.VMEM((ROWS // 2, filters * STRIP, 8 * reach), BF16),
            pltpu.VMEM(shape, BF16),
            pltpu.SemaphoreType.DMA((lats,)),
        ],
        compiler_params=pltpu.CompilerParams(vmem_limit_bytes=14 << 20),
        cost_estimate=pl.CostEstimate(
            flops=4 << 30, bytes_accessed=lats * 3 << 20, transcendentals=0
        ),
        name="bands",
    )(parity, taps, shift_table(reach))


def mix_chunks(channels):
    step = 256
    return [(o, min(step, channels - o)) for o in range(0, channels, step)]


def mixed_conv(bands, windows, mix, reach, o, w):
    conv = None
    for band, window in zip(bands, windows):
        part = jnp.dot(band, window[:, o : o + w], preferred_element_type=F32)
        conv = part if conv is None else conv + part
    total = None
    for k in range(conv.shape[0] // reach):
        part = conv[k * reach : (k + 1) * reach] * mix[k : k + 1, o : o + w].astype(F32)
        total = part if total is None else total + part
    return total


def copies(pairs, sems):
    out = [pltpu.make_async_copy(s, d, sems.at[i]) for i, (s, d) in enumerate(pairs)]
    for c in out:
        c.start()
    return out


def pre_kernel(
    need, band_in, own, above, below, near, near_halo, mix, part_out,
    own_ext, near_ext, band, part, load_sem, band_sem, out_sem,
):
    lats, reach, channels = part.shape
    loads = copies(
        [
            (above, own_ext.at[0:2]),
            (own, own_ext.at[2 : 2 + lats]),
            (below, own_ext.at[2 + lats : 3 + lats]),
            (near_halo.at[0:2], near_ext.at[0:2]),
            (near, near_ext.at[2 : 2 + lats]),
            (near_halo.at[2:3], near_ext.at[2 + lats : 3 + lats]),
        ],
        load_sem,
    )
    bands = copies([(band_in.at[a, 0:2], band.at[a]) for a in range(lats)], band_sem)
    for c in loads:
        c.wait()

    def fetched(a):
        return pltpu.make_async_copy(band_in.at[a, 0:2], band.at[a], band_sem.at[a])

    def sent(a):
        return pltpu.make_async_copy(part.at[a], part_out.at[a], out_sem.at[a])

    def one(a, carry):
        fetched(a).wait()

        @pl.when(need[a] > 0)
        def _():
            windows = [e[pl.ds(a, ROWS)].reshape(ROWS * reach, channels) for e in (own_ext, near_ext)]
            for o, w in mix_chunks(channels):
                part[a, :, o : o + w] = mixed_conv(
                    [band[a, 0], band[a, 1]], windows, mix[...], reach, o, w
                )

        @pl.when(need[a] == 0)
        def _():
            window = own_ext[pl.ds(a, ROWS)].reshape(ROWS * reach, channels)
            for o, w in mix_chunks(channels):
                part[a, :, o : o + w] = mixed_conv([band[a, 0]], [window], mix[...], reach, o, w)

        sent(a).start()
        return carry

    lax.fori_loop(0, lats, one, 0)
    for a in range(lats):
        sent(a).wait()


def conv_near(need, band, own, above, below, near, near_halo, mix):
    lats, reach, channels = own.shape
    ext = pltpu.VMEM((lats + 3, reach, channels), BF16)
    return pl.pallas_call(
        pre_kernel,
        out_shape=jax.ShapeDtypeStruct(own.shape, F32),
        in_specs=[smem(), pinned(), hbm(), hbm(), hbm(), hbm(), hbm(), vmem()],
        out_specs=hbm(),
        scratch_shapes=[
            ext,
            ext,
            pltpu.VMEM((lats, 2) + band.shape[2:], BF16),
            pltpu.VMEM(own.shape, F32),
            pltpu.SemaphoreType.DMA((6,)),
            pltpu.SemaphoreType.DMA((lats,)),
            pltpu.SemaphoreType.DMA((lats,)),
        ],
        compiler_params=pltpu.CompilerParams(vmem_limit_bytes=14 << 20),
        cost_estimate=pl.CostEstimate(
            flops=6 << 30, bytes_accessed=8 << 20, transcendentals=0
        ),
        name="conv_near",
    )(need, band, own, above, below, near, near_halo, mix)


def post_kernel(
    layer, need, band_in, far, far_halo, part_in, mix, field_in, first_in, second_in, out_ref,
    far_ext, band, part, act, field, first, second, load_sem, band_sem, part_sem, out_sem,
):
    lats, reach, channels = part.shape
    loads = copies(
        [
            (far_halo.at[0:2], far_ext.at[0:2]),
            (far, far_ext.at[2 : 2 + lats]),
            (far_halo.at[2:3], far_ext.at[2 + lats : 3 + lats]),
        ],
        load_sem,
    )
    copies([(part_in.at[a], part.at[a]) for a in range(lats)], part_sem)
    copies([(band_in.at[a, 2], band.at[a]) for a in range(lats)], band_sem)
    late = [
        pltpu.make_async_copy(s, d, load_sem.at[3 + i])
        for i, (s, d) in enumerate(
            [(first_in.at[layer], first), (second_in.at[layer], second), (field_in, field)]
        )
    ]
    for c in late:
        c.start()
    for c in loads:
        c.wait()

    def one(a, carry):
        pltpu.make_async_copy(part_in.at[a], part.at[a], part_sem.at[a]).wait()
        pltpu.make_async_copy(band_in.at[a, 2], band.at[a], band_sem.at[a]).wait()

        @pl.when(need[a] > 0)
        def _():
            window = far_ext[pl.ds(a, ROWS)].reshape(ROWS * reach, channels)
            for o, w in mix_chunks(channels):
                part[a, :, o : o + w] += mixed_conv([band[a]], [window], mix[...], reach, o, w)

        act[a] = gelu(part[a]).astype(BF16)
        return carry

    lax.fori_loop(0, lats, one, 0)
    for c in late:
        c.wait()
    half = lats // 2
    outs = []
    for h in range(2):
        rows = slice(h * half, (h + 1) * half)
        flat = act[rows].reshape(half * reach, channels)
        hidden = gelu(jnp.dot(flat, first[...], preferred_element_type=F32)).astype(BF16)
        update = jnp.dot(hidden, second[...], preferred_element_type=F32)
        field[rows] = (
            field[rows].astype(F32) + update.reshape(half, reach, channels)
        ).astype(BF16)
        c = pltpu.make_async_copy(field.at[rows], out_ref.at[rows], out_sem.at[h])
        c.start()
        outs.append(c)
    for c in outs:
        c.wait()


def finish(layer, need, band, far, far_halo, part, mix, field, first, second):
    lats, reach, channels = field.shape
    return pl.pallas_call(
        functools.partial(post_kernel, layer),
        out_shape=jax.ShapeDtypeStruct(field.shape, BF16),
        in_specs=[smem(), pinned(), hbm(), hbm(), hbm(), vmem(), hbm(), hbm(), hbm()],
        out_specs=hbm(),
        scratch_shapes=[
            pltpu.VMEM((lats + 3, reach, channels), BF16),
            pltpu.VMEM((lats,) + band.shape[2:], BF16),
            pltpu.VMEM(field.shape, F32),
            pltpu.VMEM(field.shape, BF16),
            pltpu.VMEM(field.shape, BF16),
            pltpu.VMEM(first.shape[1:], BF16),
            pltpu.VMEM(second.shape[1:], BF16),
            pltpu.SemaphoreType.DMA((6,)),
            pltpu.SemaphoreType.DMA((lats,)),
            pltpu.SemaphoreType.DMA((lats,)),
            pltpu.SemaphoreType.DMA((2,)),
        ],
        compiler_params=pltpu.CompilerParams(vmem_limit_bytes=20 << 20),
        cost_estimate=pl.CostEstimate(
            flops=5 << 30, bytes_accessed=8 << 20, transcendentals=1 << 20
        ),
        name="finish",
    )(need, band, far, far_halo, part, mix, field, first, second)


def step_route(count, distance):
    return [(i, i + distance) for i in range(count) if 0 <= i + distance < count]


def shards(grid_state, filter_taps, support_start, support_count, filter_mix, w_in, w_out):
    reach = grid_state.shape[1]
    filters = filter_taps.shape[1]
    bands_n = lax.axis_size("polar")
    ring = lax.axis_size("azimuth")
    near_route = [(i, i ^ 1) for i in range(ring)]
    far_route = [(i, (i + 1 if i % 2 else i - 1) % ring) for i in range(ring)]
    parity = lax.axis_index("azimuth") % 2
    left = (support_start < 0).astype(jnp.int32)
    right = (support_start + support_count > 1).astype(jnp.int32)
    need_near = jnp.where(parity == 0, right, left)
    need_far = jnp.where(parity == 0, left, right)
    taps = masked_rows(filter_taps, support_start, support_count, reach)
    band = make_bands(taps, parity.reshape(1), filters, reach)
    field = grid_state
    for layer in range(w_in.shape[0]):
        mix = filter_mix[layer]
        far = lax.ppermute(field, "azimuth", far_route)
        above = lax.ppermute(field[-2:], "polar", step_route(bands_n, 1))
        below = lax.ppermute(field[:1], "polar", step_route(bands_n, -1))
        near = lax.ppermute(field, "azimuth", near_route)
        halo = jnp.concatenate([above, below], axis=0)
        far_halo = lax.ppermute(halo, "azimuth", far_route)
        near_halo = lax.ppermute(halo, "azimuth", near_route)
        part = conv_near(need_near, band, field, above, below, near, near_halo, mix)
        field = finish(layer, need_far, band, far, far_halo, part, mix, field, w_in, w_out)
    return field


def solution(mesh):
    return jax.shard_map(
        shards,
        mesh=mesh,
        in_specs=(
            P("polar", "azimuth", None),
            P("polar", None, None, None),
            P("polar"),
            P("polar"),
            P(),
            P(),
            P(),
        ),
        out_specs=P("polar", "azimuth", None),
        check_vma=False,
    )
```

```python
import functools

import jax
import jax.numpy as jnp
from jax import lax
from jax.experimental import pallas as pl
from jax.experimental.pallas import tpu as pltpu
from jax.sharding import PartitionSpec as P


F32 = jnp.float32
BF16 = jnp.bfloat16
ROWS = 4
STRIP = 16


def vmem():
    return pl.BlockSpec(memory_space=pltpu.VMEM)


def smem():
    return pl.BlockSpec(memory_space=pltpu.SMEM)


def gelu(x):
    return 0.5 * x * (1.0 + lax.erf(x * 0.7071067811865476))


def shift_table(reach):
    wide, strips = 4 * reach, reach // STRIP
    column = jnp.arange(3 * strips * 2 * reach, dtype=jnp.int32)
    section, strip = column // (strips * 2 * reach), column // (2 * reach) % strips
    lane = column % (2 * reach)
    tap = (section * reach - STRIP * strip + lane % reach) % wide
    source = lane // reach * wide + tap
    return (jnp.arange(2 * wide, dtype=jnp.int32)[:, None] == source[None, :]).astype(BF16)


def band_kernel(reach, parity, first, count, taps, table, band, rows, base):
    lats, filters, _, tap_count = taps.shape
    wide, strips = 4 * reach, reach // STRIP
    span = strips * 2 * reach
    order = [2 - parity[0], 0, 1 + parity[0]]
    rows[...] = jnp.zeros_like(rows)
    lane = lax.broadcasted_iota(jnp.int32, (ROWS, tap_count), 1) - reach

    def one(a, carry):
        inside = (lane >= first[a]) & (lane < first[a] + count[a])
        for k in range(filters):
            rows[k, 0:ROWS, 0:tap_count] = jnp.where(inside, taps[a, k].astype(F32), 0.0)
        for k in range(filters):
            for r in range(ROWS):
                skew = pltpu.roll(
                    jnp.broadcast_to(rows[k, r : r + 1, :], (STRIP, wide)),
                    0, 1, stride=1, stride_axis=0,
                )
                base[r // 2, k * STRIP : (k + 1) * STRIP, r % 2 * wide : (r % 2 + 1) * wide] = (
                    skew.astype(BF16)
                )
        for pair in range(ROWS // 2):
            for s in range(3):
                rolled = jnp.dot(
                    base[pair], table[:, s * span : (s + 1) * span], preferred_element_type=F32
                ).astype(BF16)
                for k in range(filters):
                    for b in range(strips):
                        row = k * reach + STRIP * b
                        band[
                            a,
                            order[s],
                            row : row + STRIP,
                            pair * 2 * reach : (pair + 1) * 2 * reach,
                        ] = rolled[k * STRIP : (k + 1) * STRIP, b * 2 * reach : (b + 1) * 2 * reach]
        return carry

    lax.fori_loop(0, lats, one, 0)


def make_bands(parity, first, count, taps, reach):
    lats, filters = taps.shape[:2]
    shape = (lats, 3, filters * reach, ROWS * reach)
    return pl.pallas_call(
        functools.partial(band_kernel, reach),
        out_shape=jax.ShapeDtypeStruct(shape, BF16),
        in_specs=[smem(), smem(), smem(), vmem(), vmem()],
        out_specs=vmem(),
        scratch_shapes=[
            pltpu.VMEM((filters, 8, 4 * reach), F32),
            pltpu.VMEM((ROWS // 2, filters * STRIP, 8 * reach), BF16),
        ],
        compiler_params=pltpu.CompilerParams(vmem_limit_bytes=10 << 20),
        cost_estimate=pl.CostEstimate(
            flops=4 << 30, bytes_accessed=lats * 3 << 20, transcendentals=0
        ),
        name="bands",
    )(parity, first, count, taps, shift_table(reach))


def mix_chunks(channels):
    step = 256
    return [(o, min(step, channels - o)) for o in range(0, channels, step)]


def convolve(bands, windows, conv, o, w):
    total = None
    for band, window in zip(bands, windows):
        part = jnp.dot(band, window[:, o : o + w], preferred_element_type=F32)
        total = part if total is None else total + part
    conv[:, o : o + w] = total


def mixed(conv, mix, reach, o, w):
    total = None
    for k in range(mix.shape[0]):
        part = conv[k * reach : (k + 1) * reach, o : o + w] * mix[k : k + 1, o : o + w].astype(F32)
        total = part if total is None else total + part
    return total


def extend(ext, above, own, below):
    lats = own.shape[0]
    ext[0:2] = above
    ext[2 : 2 + lats] = own
    ext[2 + lats : 3 + lats] = below


def pipelined(lats, fill, drain):
    def pair(i, carry):
        fill(2 * i, 0, jnp.maximum(2 * i - 1, 0), 1)
        fill(2 * i + 1, 1, 2 * i, 0)
        return carry

    lax.fori_loop(0, lats // 2, pair, 0)
    drain(lats - 1, 1)


def pre_kernel(
    layer, parity, first, count, band, own, above, below, near, near_halo, mixes, part,
    own_ext, near_ext, conv,
):
    lats, reach, channels = part.shape
    mix = mixes.at[layer]
    extend(own_ext, above[...], own[...], below[...])
    extend(near_ext, near_halo[0:2], near[...], near_halo[2:3])
    conv[1] = jnp.zeros_like(conv[1])

    def drain(a, slot, o=0, w=channels):
        part[a, :, o : o + w] = mixed(conv.at[slot], mix, reach, o, w)

    def fill(a, slot, last, other):
        def with_bands(exts):
            windows = [e[pl.ds(a, ROWS)].reshape(ROWS * reach, channels) for e in exts]
            bands = [band[a, s] for s in range(len(exts))]
            for o, w in mix_chunks(channels):
                convolve(bands, windows, conv.at[slot], o, w)
                drain(last, other, o, w)

        need = jnp.where(parity[0] == 0, (first[a] + count[a] > 1), (first[a] < 0))

        @pl.when(need)
        def _():
            with_bands([own_ext, near_ext])

        @pl.when(jnp.logical_not(need))
        def _():
            with_bands([own_ext])

    pipelined(lats, fill, drain)


def conv_near(layer, scalars, band, own, above, below, near, near_halo, mixes):
    lats, reach, channels = own.shape
    ext = pltpu.VMEM((lats + 3, reach, channels), BF16)
    return pl.pallas_call(
        functools.partial(pre_kernel, layer),
        out_shape=jax.ShapeDtypeStruct(own.shape, F32),
        in_specs=[smem()] * 3 + [vmem()] * 7,
        out_specs=vmem(),
        scratch_shapes=[ext, ext, pltpu.VMEM((2, band.shape[2], channels), F32)],
        compiler_params=pltpu.CompilerParams(vmem_limit_bytes=10 << 20),
        cost_estimate=pl.CostEstimate(
            flops=6 << 30, bytes_accessed=8 << 20, transcendentals=0
        ),
        name="conv_near",
    )(*scalars, band, own, above, below, near, near_halo, mixes)


def post_kernel(
    layer, band, far, far_halo, part, mixes, field, first, second, out,
    far_ext, conv, act, hidden,
):
    lats, reach, channels = part.shape
    mix = mixes.at[layer]
    extend(far_ext, far_halo[0:2], far[...], far_halo[2:3])
    conv[1] = jnp.zeros_like(conv[1])

    def drain(a, slot, o=0, w=channels):
        total = part[a, :, o : o + w] + mixed(conv.at[slot], mix, reach, o, w)
        act[pl.ds(pl.multiple_of(a * reach, reach), reach), o : o + w] = gelu(total).astype(BF16)

    def fill(a, slot, last, other):
        window = far_ext[pl.ds(a, ROWS)].reshape(ROWS * reach, channels)
        for o, w in mix_chunks(channels):
            convolve([band[a, 2]], [window], conv.at[slot], o, w)
            drain(last, other, o, w)

    pipelined(lats, fill, drain)
    for o, w in mix_chunks(first.shape[2]):
        up = jnp.dot(act[...], first[layer, :, o : o + w], preferred_element_type=F32)
        hidden[:, o : o + w] = gelu(up).astype(BF16)
    for o, w in mix_chunks(channels):
        update = jnp.dot(hidden[...], second[layer, :, o : o + w], preferred_element_type=F32)
        out[:, :, o : o + w] = (
            field[:, :, o : o + w].astype(F32) + update.reshape(lats, reach, w)
        ).astype(BF16)


def finish(layer, band, far, far_halo, part, mixes, field, first, second):
    lats, reach, channels = field.shape
    return pl.pallas_call(
        functools.partial(post_kernel, layer),
        out_shape=jax.ShapeDtypeStruct(field.shape, BF16),
        in_specs=[vmem()] * 8,
        out_specs=vmem(),
        scratch_shapes=[
            pltpu.VMEM((lats + 3, reach, channels), BF16),
            pltpu.VMEM((2, band.shape[2], channels), F32),
            pltpu.VMEM((lats * reach, channels), BF16),
            pltpu.VMEM((lats * reach, first.shape[2]), BF16),
        ],
        compiler_params=pltpu.CompilerParams(vmem_limit_bytes=14 << 20),
        cost_estimate=pl.CostEstimate(
            flops=5 << 30, bytes_accessed=8 << 20, transcendentals=1 << 20
        ),
        name="finish",
    )(band, far, far_halo, part, mixes, field, first, second)


def step_route(count, distance):
    return [(i, i + distance) for i in range(count) if 0 <= i + distance < count]


def shards(grid_state, filter_taps, support_start, support_count, filter_mix, w_in, w_out):
    reach = grid_state.shape[1]
    polar = lax.axis_size("polar")
    ring = lax.axis_size("azimuth")
    near_route = [(i, i ^ 1) for i in range(ring)]
    far_route = [(i, (i + 1 if i % 2 else i - 1) % ring) for i in range(ring)]
    parity = lax.rem(lax.axis_index("azimuth"), 2).reshape(1)
    scalars = (parity, support_start, support_count)
    band = make_bands(*scalars, filter_taps, reach)
    field = grid_state
    for layer in range(w_in.shape[0]):
        far = lax.ppermute(field, "azimuth", far_route)
        near = lax.ppermute(field, "azimuth", near_route)
        above = lax.ppermute(field[-2:], "polar", step_route(polar, 1))
        below = lax.ppermute(field[:1], "polar", step_route(polar, -1))
        halo = jnp.concatenate([above, below], axis=0)
        far_halo = lax.ppermute(halo, "azimuth", far_route)
        near_halo = lax.ppermute(halo, "azimuth", near_route)
        part = conv_near(
            layer, scalars, band, field, above, below, near, near_halo, filter_mix
        )
        field = finish(layer, band, far, far_halo, part, filter_mix, field, w_in, w_out)
    return field


def solution(mesh):
    return jax.shard_map(
        shards,
        mesh=mesh,
        in_specs=(
            P("polar", "azimuth", None),
            P("polar", None, None, None),
            P("polar"),
            P("polar"),
            P(),
            P(),
            P(),
        ),
        out_specs=P("polar", "azimuth", None),
        check_vma=False,
    )
```

```python
import functools

import jax
import jax.numpy as jnp
from jax import lax
from jax.experimental import pallas as pl
from jax.experimental.pallas import tpu as pltpu
from jax.sharding import PartitionSpec as P


F32 = jnp.float32
BF16 = jnp.bfloat16
ROWS = 4
STRIP = 16


def vmem():
    return pl.BlockSpec(memory_space=pltpu.VMEM)


def smem():
    return pl.BlockSpec(memory_space=pltpu.SMEM)


def gelu(x):
    return 0.5 * x * (1.0 + lax.erf(x * 0.7071067811865476))


def shift_tables(reach):
    wide, strips = 4 * reach, reach // STRIP
    column = jnp.arange(3 * strips * reach, dtype=jnp.int32)[None, :]
    odd = jnp.arange(2, dtype=jnp.int32)[:, None]
    section, strip = column // (strips * reach), column // reach % strips
    strip = strip + odd * (1 - 2 * (strip % 2))
    tap = (section * reach - STRIP * strip + column % reach) % wide
    return (jnp.arange(wide, dtype=jnp.int32)[None, :, None] == tap[:, None, :]).astype(BF16)


def band_kernel(reach, info, taps, table, band, rows, base):
    lats, filters, _, tap_count = taps.shape
    wide, strips = 4 * reach, reach // STRIP
    parity = info[2 * lats]
    order = [2 - parity, 0, 1 + parity]
    block = filters * STRIP
    rows[...] = jnp.zeros_like(rows)
    lane = lax.broadcasted_iota(jnp.int32, (ROWS, tap_count), 1) - reach

    def skewed(a, carry):
        inside = (lane >= info[a]) & (lane < info[a] + info[lats + a])
        for k in range(filters):
            rows[k, 0:ROWS, 0:tap_count] = jnp.where(inside, taps[a, k].astype(F32), 0.0)
        for k in range(filters):
            at = pl.ds(pl.multiple_of(a * block + k * STRIP, STRIP), STRIP)
            for r in range(ROWS):
                skew = pltpu.roll(
                    jnp.broadcast_to(rows[k, r : r + 1, :], (STRIP, wide)),
                    0, 1, stride=1, stride_axis=0,
                )
                base[r, at, :] = skew.astype(BF16)
        return carry

    lax.fori_loop(0, lats, skewed, 0)
    low = lax.broadcasted_iota(jnp.int32, (lats * block, 2 * reach), 1) < reach
    for s in range(3):
        columns = slice(s * strips * reach, (s + 1) * strips * reach)
        for pair in range(ROWS // 2):
            even, odd = (
                jnp.dot(base[2 * pair + m], table[m, :, columns], preferred_element_type=F32).astype(BF16)
                for m in range(2)
            )
            for b in range(0, strips, 2):
                e, o = (x[:, b * reach : (b + 2) * reach] for x in (even, odd))
                joined = [jnp.where(low, e, o), pltpu.roll(jnp.where(low, o, e), reach, 1)]
                for c in range(2):
                    for a in range(lats):
                        for k in range(filters):
                            at = k * reach + STRIP * (b + c)
                            row = a * block + k * STRIP
                            band[
                                a,
                                order[s],
                                at : at + STRIP,
                                pair * 2 * reach : (pair + 1) * 2 * reach,
                            ] = joined[c][row : row + STRIP]


def make_bands(info, taps, reach):
    lats, filters = taps.shape[:2]
    shape = (lats, 3, filters * reach, ROWS * reach)
    return pl.pallas_call(
        functools.partial(band_kernel, reach),
        out_shape=jax.ShapeDtypeStruct(shape, BF16),
        in_specs=[smem(), vmem(), vmem()],
        out_specs=vmem(),
        scratch_shapes=[
            pltpu.VMEM((filters, 8, 4 * reach), F32),
            pltpu.VMEM((ROWS, lats * filters * STRIP, 4 * reach), BF16),
        ],
        compiler_params=pltpu.CompilerParams(vmem_limit_bytes=12 << 20),
        cost_estimate=pl.CostEstimate(
            flops=4 << 30, bytes_accessed=lats * 3 << 20, transcendentals=0
        ),
        name="bands",
    )(info, taps, shift_tables(reach))


def split_rows(rows, down, up, edge, body):
    lats = rows.shape[0]
    top, rest, end = pl.ds(0, 1), pl.ds(1, lats - 3), pl.ds(lats - 2, 2)
    return [
        (rows.at[end], down),
        (rows.at[top], up),
        (rows.at[end], edge.at[pl.ds(0, 2)]),
        (rows.at[top], edge.at[pl.ds(2, 1)]),
        (rows.at[rest], body),
    ]


def fetch_kernel(field, taps, down, up, edge, body, taps_out, sem):
    moves = split_rows(field, down, up, edge, body) + [(taps, taps_out)]
    moves = [pltpu.make_async_copy(s, d, sem.at[i]) for i, (s, d) in enumerate(moves)]
    for m in moves:
        m.start()
    for m in moves:
        m.wait()


def fetch(field, taps):
    shapes = [(n,) + field.shape[1:] for n in (2, 1, 3, field.shape[0] - 3)] + [taps.shape]
    return pl.pallas_call(
        fetch_kernel,
        out_shape=[jax.ShapeDtypeStruct(s, BF16) for s in shapes],
        in_specs=[pl.BlockSpec(memory_space=pl.ANY)] * 2,
        out_specs=[vmem()] * len(shapes),
        scratch_shapes=[pltpu.SemaphoreType.DMA((6,))],
        compiler_params=pltpu.CompilerParams(vmem_limit_bytes=60 << 20),
        cost_estimate=pl.CostEstimate(flops=0, bytes_accessed=1 << 20, transcendentals=0),
        name="fetch",
    )(field, taps)


def mix_chunks(channels):
    step = 256
    return [(o, min(step, channels - o)) for o in range(0, channels, step)]


def convolve(bands, windows, conv, o, w):
    total = None
    for band, window in zip(bands, windows):
        part = jnp.dot(band, window[:, o : o + w], preferred_element_type=F32)
        total = part if total is None else total + part
    conv[:, o : o + w] = total


def mixed(conv, mixes, layer, reach, o, w):
    total = None
    for k in range(mixes.shape[0]):
        mix = mixes[k, layer : layer + 1, o : o + w].astype(F32)
        part = conv[k * reach : (k + 1) * reach, o : o + w] * mix
        total = part if total is None else total + part
    return total


def local_kernel(layer, inner, info, band, *refs):
    if inner:
        own, near, mixes, part, conv = refs
        halos = (None, None)
    else:
        own, own_halo, near, near_halo, mixes, part, conv = refs
        halos = (own_halo, near_halo)
    lats, reach, channels = own.shape

    def drain(p, slot, o=0, w=channels):
        part[p, :, o : o + w] = mixed(conv.at[slot], mixes, layer, reach, o, w)

    def fill(a, slot, last):
        def window(block, halo):
            if inner:
                rows = block[pl.ds(a - 2, ROWS)]
            elif a < 2:
                rows = jnp.concatenate([halo[a:2], block[0 : a + 2]], axis=0)
            else:
                rows = jnp.concatenate([block[a - 2 : lats], halo[2:3]], axis=0)
            return rows.reshape(ROWS * reach, channels)

        def with_sections(blocks):
            windows = [window(b, h) for b, h in zip(blocks, halos)]
            bands = [band[a, s] for s in range(len(blocks))]
            for o, w in mix_chunks(channels):
                convolve(bands, windows, conv.at[slot], o, w)
                if last is not None:
                    drain(last, 1 - slot, o, w)

        need = jnp.where(info[2 * lats] == 0, info[a] + info[lats + a] > 1, info[a] < 0)

        @pl.when(need)
        def _():
            with_sections([own, near])

        @pl.when(jnp.logical_not(need))
        def _():
            with_sections([own])

    count = part.shape[0]
    if inner:
        looped = count // 2 * 2

        def pair(i, carry):
            fill(2 * i + 2, 0, jnp.maximum(2 * i - 1, 0))
            fill(2 * i + 3, 1, 2 * i)
            return carry

        lax.fori_loop(0, looped // 2, pair, 0)
        for p in range(looped, count):
            fill(p + 2, 0, p - 1)
    else:
        for p, a in enumerate((0, 1, lats - 1)):
            fill(a, p % 2, p - 1 if p else None)
    drain(count - 1, (count - 1) % 2)


def conv_local(layer, info, band, own, near, mixes, halos=None):
    lats, reach, channels = own.shape
    inner = halos is None
    count = lats - 3 if inner else 3
    blocks = (own, near) if inner else (own, halos[0], near, halos[1])
    return pl.pallas_call(
        functools.partial(local_kernel, layer, inner),
        out_shape=jax.ShapeDtypeStruct((count, reach, channels), F32),
        in_specs=[smem()] + [vmem()] * (len(blocks) + 2),
        out_specs=vmem(),
        scratch_shapes=[pltpu.VMEM((2, band.shape[2], channels), F32)],
        compiler_params=pltpu.CompilerParams(vmem_limit_bytes=10 << 20),
        cost_estimate=pl.CostEstimate(
            flops=count << 29, bytes_accessed=count << 20, transcendentals=0
        ),
        name="conv_inner" if inner else "conv_outer",
    )(info, band, *blocks, mixes)


def post_kernel(
    layer, band, far_edge, far_body, far_halo, part_inner, part_outer, mixes, field, first, second, out, *edges_and_scratch
):
    edges, (far_ext, conv, act, hidden) = edges_and_scratch[:-4], edges_and_scratch[-4:]
    lats, reach, channels = field.shape
    far_ext[0:2] = far_halo[0:2]
    far_ext[2:3] = far_edge[2:3]
    far_ext[3:lats] = far_body[...]
    far_ext[lats : lats + 2] = far_edge[0:2]
    far_ext[lats + 2 : lats + 3] = far_halo[2:3]
    inner = lats - 3
    outer = (0, 1, lats - 1)

    def lat_of(p):
        return p + 2 if not isinstance(p, int) or p < inner else outer[p - inner]

    def drain(p, slot, o=0, w=channels):
        part = part_inner if not isinstance(p, int) or p < inner else part_outer.at[pl.ds(p - inner, 1)]
        at = p if part is part_inner else 0
        total = part[at, :, o : o + w] + mixed(conv.at[slot], mixes, layer, reach, o, w)
        row = lat_of(p) * reach
        row = row if isinstance(row, int) else pl.multiple_of(row, reach)
        act[pl.ds(row, reach), o : o + w] = gelu(total).astype(BF16)

    def fill(p, slot, last):
        a = lat_of(p)
        window = far_ext[pl.ds(a, ROWS)].reshape(ROWS * reach, channels)
        for o, w in mix_chunks(channels):
            convolve([band[a, 2]], [window], conv.at[slot], o, w)
            drain(last, 1 - slot, o, w)

    def pair(i, carry):
        fill(2 * i, 0, jnp.maximum(2 * i - 1, 0))
        fill(2 * i + 1, 1, 2 * i)
        return carry

    looped = inner // 2 * 2
    lax.fori_loop(0, looped // 2, pair, 0)
    for p in range(looped, lats):
        fill(p, p % 2, p - 1)
    drain(lats - 1, (lats - 1) % 2)
    for o, w in mix_chunks(first.shape[2]):
        up = jnp.dot(act[...], first[layer, :, o : o + w], preferred_element_type=F32)
        hidden[:, o : o + w] = gelu(up).astype(BF16)
    for o, w in mix_chunks(channels):
        update = jnp.dot(hidden[...], second[layer, :, o : o + w], preferred_element_type=F32)
        out[:, :, o : o + w] = (
            field[:, :, o : o + w].astype(F32) + update.reshape(lats, reach, w)
        ).astype(BF16)
    if edges:
        for source, target in split_rows(out, *edges):
            target[...] = source[...]


def finish(layer, last, band, far_edge, far_body, far_halo, parts, mixes, field, first, second):
    lats, reach, channels = field.shape
    counts = [lats] if last else [lats, 2, 1, 3, lats - 3]
    return pl.pallas_call(
        functools.partial(post_kernel, layer),
        out_shape=[jax.ShapeDtypeStruct((n, reach, channels), BF16) for n in counts],
        in_specs=[vmem()] * 10,
        out_specs=[vmem()] * len(counts),
        scratch_shapes=[
            pltpu.VMEM((lats + 3, reach, channels), BF16),
            pltpu.VMEM((2, band.shape[2], channels), F32),
            pltpu.VMEM((lats * reach, channels), BF16),
            pltpu.VMEM((lats * reach, first.shape[2]), BF16),
        ],
        compiler_params=pltpu.CompilerParams(vmem_limit_bytes=14 << 20),
        cost_estimate=pl.CostEstimate(
            flops=5 << 30, bytes_accessed=8 << 20, transcendentals=1 << 20
        ),
        name="finish",
    )(band, far_edge, far_body, far_halo, *parts, mixes, field, first, second)


def shards(grid_state, filter_taps, support_start, support_count, filter_mix, w_in, w_out):
    reach = grid_state.shape[1]
    layers = w_in.shape[0]
    polar, ring = lax.axis_size("polar"), lax.axis_size("azimuth")
    near_route = [(i, i ^ 1) for i in range(ring)]
    far_route = [(i, (i + 1 if i % 2 else i - 1) % ring) for i in range(ring)]
    down_route = [(i, (i + 1) % polar) for i in range(polar)]
    up_route = [(i, (i - 1) % polar) for i in range(polar)]
    here = lax.axis_index("polar")
    parity = lax.rem(lax.axis_index("azimuth"), 2).reshape(1)
    info = jnp.concatenate([support_start, support_count, parity])

    def halo_of(above, below):
        above = jnp.where(here > 0, above, jnp.zeros_like(above))
        below = jnp.where(here < polar - 1, below, jnp.zeros_like(below))
        return jnp.concatenate([above, below], axis=0)

    mixes = jnp.transpose(filter_mix, (1, 0, 2))
    field = grid_state
    down, up, edge, body, taps = fetch(field, filter_taps)
    for layer in range(layers):
        far_edge = lax.ppermute(edge, "azimuth", far_route)
        far_body = lax.ppermute(body, "azimuth", far_route)
        near = lax.ppermute(field, "azimuth", near_route)
        above = lax.ppermute(down, "polar", down_route)
        below = lax.ppermute(up, "polar", up_route)
        if layer == 0:
            band = make_bands(info, taps, reach)
        inner = conv_local(layer, info, band, field, near, mixes)
        far_above = lax.ppermute(far_edge[:2], "polar", down_route)
        far_below = lax.ppermute(far_edge[2:], "polar", up_route)
        halo = halo_of(above, below)
        near_halo = lax.ppermute(halo, "azimuth", near_route)
        outer = conv_local(layer, info, band, field, near, mixes, (halo, near_halo))
        out = finish(
            layer, layer == layers - 1, band, far_edge, far_body,
            halo_of(far_above, far_below), (inner, outer), mixes, field, w_in, w_out,
        )
        field, (down, up, edge, body) = out[0], out[1:] or (None,) * 4
    return field


def solution(mesh):
    return jax.shard_map(
        shards,
        mesh=mesh,
        in_specs=(
            P("polar", "azimuth", None),
            P("polar", None, None, None),
            P("polar"),
            P("polar"),
            P(),
            P(),
            P(),
        ),
        out_specs=P("polar", "azimuth", None),
        check_vma=False,
    )
```

```python
import functools

import jax
import jax.numpy as jnp
from jax import lax
from jax.experimental import pallas as pl
from jax.experimental.pallas import tpu as pltpu
from jax.sharding import PartitionSpec as P


F32 = jnp.float32
BF16 = jnp.bfloat16
ROWS = 4
STRIP = 16


def vmem():
    return pl.BlockSpec(memory_space=pltpu.VMEM)


def smem():
    return pl.BlockSpec(memory_space=pltpu.SMEM)


def gelu(x):
    return 0.5 * x * (1.0 + lax.erf(x * 0.7071067811865476))


def shift_tables(reach):
    wide, strips = 4 * reach, reach // STRIP
    column = jnp.arange(3 * strips * reach, dtype=jnp.int32)[None, :]
    odd = jnp.arange(2, dtype=jnp.int32)[:, None]
    section, strip = column // (strips * reach), column // reach % strips
    strip = strip + odd * (1 - 2 * (strip % 2))
    tap = (section * reach - STRIP * strip + column % reach) % wide
    return (jnp.arange(wide, dtype=jnp.int32)[None, :, None] == tap[:, None, :]).astype(BF16)


def band_kernel(reach, info, taps, table, band, rows, base):
    lats, filters, _, tap_count = taps.shape
    wide, strips = 4 * reach, reach // STRIP
    parity = info[2 * lats]
    order = [2 - parity, 0, 1 + parity]
    block = filters * STRIP
    rows[...] = jnp.zeros_like(rows)
    lane = lax.broadcasted_iota(jnp.int32, (ROWS, tap_count), 1) - reach

    def masked(a, carry):
        inside = (lane >= info[a]) & (lane < info[a] + info[lats + a])
        for k in range(filters):
            rows[a, k, 0:ROWS, 0:tap_count] = jnp.where(inside, taps[a, k].astype(F32), 0.0)
        return carry

    lax.fori_loop(0, lats, masked, 0)

    def skew(r):
        for a in range(lats):
            for k in range(filters):
                at = a * block + k * STRIP
                row = jnp.broadcast_to(rows[a, k, r : r + 1, :], (STRIP, wide))
                base[r, at : at + STRIP, :] = pltpu.roll(row, 0, 1, stride=1, stride_axis=0).astype(BF16)

    low = lax.broadcasted_iota(jnp.int32, (lats * block, 2 * reach), 1) < reach
    for pair in range(ROWS // 2):
        skew(2 * pair)
        skew(2 * pair + 1)
        for s in range(3):
            columns = slice(s * strips * reach, (s + 1) * strips * reach)
            even, odd = (
                jnp.dot(base[2 * pair + m], table[m, :, columns], preferred_element_type=F32).astype(BF16)
                for m in range(2)
            )
            for b in range(0, strips, 2):
                e, o = (x[:, b * reach : (b + 2) * reach] for x in (even, odd))
                joined = [jnp.where(low, e, o), pltpu.roll(jnp.where(low, o, e), reach, 1)]
                for c in range(2):
                    for a in range(lats):
                        for k in range(filters):
                            at = k * reach + STRIP * (b + c)
                            row = a * block + k * STRIP
                            band[
                                a,
                                order[s],
                                at : at + STRIP,
                                pair * 2 * reach : (pair + 1) * 2 * reach,
                            ] = joined[c][row : row + STRIP]


def make_bands(info, taps, reach):
    lats, filters = taps.shape[:2]
    shape = (lats, 3, filters * reach, ROWS * reach)
    return pl.pallas_call(
        functools.partial(band_kernel, reach),
        out_shape=jax.ShapeDtypeStruct(shape, BF16),
        in_specs=[smem(), vmem(), vmem()],
        out_specs=vmem(),
        scratch_shapes=[
            pltpu.VMEM((lats, filters, 8, 4 * reach), F32),
            pltpu.VMEM((ROWS, lats * filters * STRIP, 4 * reach), BF16),
        ],
        compiler_params=pltpu.CompilerParams(vmem_limit_bytes=12 << 20),
        cost_estimate=pl.CostEstimate(
            flops=4 << 30, bytes_accessed=lats * 3 << 20, transcendentals=0
        ),
        name="bands",
    )(info, taps, shift_tables(reach))


def split_rows(rows, down, up, edge, body):
    lats = rows.shape[0]
    top, rest, end = pl.ds(0, 1), pl.ds(1, lats - 3), pl.ds(lats - 2, 2)
    return [
        (rows.at[end], down),
        (rows.at[top], up),
        (rows.at[end], edge.at[pl.ds(0, 2)]),
        (rows.at[top], edge.at[pl.ds(2, 1)]),
        (rows.at[rest], body),
    ]


def fetch_kernel(field, down, up, edge, body, sem):
    moves = split_rows(field, down, up, edge, body)
    moves = [pltpu.make_async_copy(s, d, sem.at[i]) for i, (s, d) in enumerate(moves)]
    for m in moves:
        m.start()
    for m in moves:
        m.wait()


def fetch(field):
    shapes = [(n,) + field.shape[1:] for n in (2, 1, 3, field.shape[0] - 3)]
    return pl.pallas_call(
        fetch_kernel,
        out_shape=[jax.ShapeDtypeStruct(s, BF16) for s in shapes],
        in_specs=[pl.BlockSpec(memory_space=pl.ANY)],
        out_specs=[vmem()] * len(shapes),
        scratch_shapes=[pltpu.SemaphoreType.DMA((5,))],
        compiler_params=pltpu.CompilerParams(vmem_limit_bytes=4 << 20),
        cost_estimate=pl.CostEstimate(flops=0, bytes_accessed=1 << 20, transcendentals=0),
        name="fetch",
    )(field)


def mix_chunks(channels):
    step = 256
    return [(o, min(step, channels - o)) for o in range(0, channels, step)]


def convolve(bands, windows, conv, o, w):
    total = None
    for band, window in zip(bands, windows):
        part = jnp.dot(band, window[:, o : o + w], preferred_element_type=F32)
        total = part if total is None else total + part
    conv[:, o : o + w] = total


def mixed(conv, mixes, layer, reach, o, w):
    total = None
    for k in range(mixes.shape[0]):
        mix = mixes[k, layer : layer + 1, o : o + w].astype(F32)
        part = conv[k * reach : (k + 1) * reach, o : o + w] * mix
        total = part if total is None else total + part
    return total


def local_kernel(layer, inner, info, band, *refs):
    if inner:
        own, near, mixes, part, conv = refs
        halos = (None, None)
    else:
        own, own_halo, near, near_halo, mixes, part, conv = refs
        halos = (own_halo, near_halo)
    lats, reach, channels = own.shape

    def drain(p, slot, o=0, w=channels):
        part[p, :, o : o + w] = mixed(conv.at[slot], mixes, layer, reach, o, w)

    def fill(a, slot, last):
        def window(block, halo):
            if inner:
                rows = block[pl.ds(a - 2, ROWS)]
            elif a < 2:
                rows = jnp.concatenate([halo[a:2], block[0 : a + 2]], axis=0)
            else:
                rows = jnp.concatenate([block[a - 2 : lats], halo[2:3]], axis=0)
            return rows.reshape(ROWS * reach, channels)

        def with_sections(blocks):
            windows = [window(b, h) for b, h in zip(blocks, halos)]
            bands = [band[a, s] for s in range(len(blocks))]
            for o, w in mix_chunks(channels):
                convolve(bands, windows, conv.at[slot], o, w)
                if last is not None:
                    drain(last, 1 - slot, o, w)

        need = jnp.where(info[2 * lats] == 0, info[a] + info[lats + a] > 1, info[a] < 0)

        @pl.when(need)
        def _():
            with_sections([own, near])

        @pl.when(jnp.logical_not(need))
        def _():
            with_sections([own])

    count = part.shape[0]
    if inner:
        looped = count // 2 * 2

        def pair(i, carry):
            fill(2 * i + 2, 0, jnp.maximum(2 * i - 1, 0))
            fill(2 * i + 3, 1, 2 * i)
            return carry

        lax.fori_loop(0, looped // 2, pair, 0)
        for p in range(looped, count):
            fill(p + 2, 0, p - 1)
    else:
        for p, a in enumerate((0, 1, lats - 1)):
            fill(a, p % 2, p - 1 if p else None)
    drain(count - 1, (count - 1) % 2)


def conv_local(layer, info, band, own, near, mixes, halos=None):
    lats, reach, channels = own.shape
    inner = halos is None
    count = lats - 3 if inner else 3
    blocks = (own, near) if inner else (own, halos[0], near, halos[1])
    return pl.pallas_call(
        functools.partial(local_kernel, layer, inner),
        out_shape=jax.ShapeDtypeStruct((count, reach, channels), F32),
        in_specs=[smem()] + [vmem()] * (len(blocks) + 2),
        out_specs=vmem(),
        scratch_shapes=[pltpu.VMEM((2, band.shape[2], channels), F32)],
        compiler_params=pltpu.CompilerParams(vmem_limit_bytes=10 << 20),
        cost_estimate=pl.CostEstimate(
            flops=count << 29, bytes_accessed=count << 20, transcendentals=0
        ),
        name="conv_inner" if inner else "conv_outer",
    )(info, band, *blocks, mixes)


def post_kernel(
    layer, last, band, far_edge, far_body, far_halo, part_inner, part_outer, mixes, field, first, second, result, *edges_and_scratch
):
    edges = edges_and_scratch[: 0 if last else 4]
    far_ext, conv, act, hidden, *rest = edges_and_scratch[len(edges) :]
    out, sent = rest if last else (result, None)
    lats, reach, channels = field.shape
    far_ext[0:2] = far_halo[0:2]
    far_ext[2:3] = far_edge[2:3]
    far_ext[3:lats] = far_body[...]
    far_ext[lats : lats + 2] = far_edge[0:2]
    far_ext[lats + 2 : lats + 3] = far_halo[2:3]
    inner = lats - 3
    outer = (0, 1, lats - 1)

    def lat_of(p):
        return p + 2 if not isinstance(p, int) or p < inner else outer[p - inner]

    def drain(p, slot, o=0, w=channels):
        part = part_inner if not isinstance(p, int) or p < inner else part_outer.at[pl.ds(p - inner, 1)]
        at = p if part is part_inner else 0
        total = part[at, :, o : o + w] + mixed(conv.at[slot], mixes, layer, reach, o, w)
        row = lat_of(p) * reach
        row = row if isinstance(row, int) else pl.multiple_of(row, reach)
        act[pl.ds(row, reach), o : o + w] = gelu(total).astype(BF16)

    def fill(p, slot, last):
        a = lat_of(p)
        window = far_ext[pl.ds(a, ROWS)].reshape(ROWS * reach, channels)
        for o, w in mix_chunks(channels):
            convolve([band[a, 2]], [window], conv.at[slot], o, w)
            drain(last, 1 - slot, o, w)

    def pair(i, carry):
        fill(2 * i, 0, jnp.maximum(2 * i - 1, 0))
        fill(2 * i + 1, 1, 2 * i)
        return carry

    looped = inner // 2 * 2
    lax.fori_loop(0, looped // 2, pair, 0)
    for p in range(looped, lats):
        fill(p, p % 2, p - 1)
    drain(lats - 1, (lats - 1) % 2)
    for o, w in mix_chunks(first.shape[2]):
        up = jnp.dot(act[...], first[layer, :, o : o + w], preferred_element_type=F32)
        hidden[:, o : o + w] = gelu(up).astype(BF16)
    sends = []
    for o, w in mix_chunks(channels):
        update = jnp.dot(hidden[...], second[layer, :, o : o + w], preferred_element_type=F32)
        out[:, :, o : o + w] = (
            field[:, :, o : o + w].astype(F32) + update.reshape(lats, reach, w)
        ).astype(BF16)
        if last:
            part = (slice(None), slice(None), pl.ds(o, w))
            sends.append(pltpu.make_async_copy(out.at[part], result.at[part], sent.at[len(sends)]))
            sends[-1].start()
    for send in sends:
        send.wait()
    if edges:
        for source, target in split_rows(out, *edges):
            target[...] = source[...]


def finish(layer, last, band, far_edge, far_body, far_halo, parts, mixes, field, first, second):
    lats, reach, channels = field.shape
    counts = [lats] if last else [lats, 2, 1, 3, lats - 3]
    return pl.pallas_call(
        functools.partial(post_kernel, layer, last),
        out_shape=[jax.ShapeDtypeStruct((n, reach, channels), BF16) for n in counts],
        in_specs=[vmem()] * 10,
        out_specs=[pl.BlockSpec(memory_space=pl.ANY)] if last else [vmem()] * len(counts),
        scratch_shapes=[
            pltpu.VMEM((lats + 3, reach, channels), BF16),
            pltpu.VMEM((2, band.shape[2], channels), F32),
            pltpu.VMEM((lats * reach, channels), BF16),
            pltpu.VMEM((lats * reach, first.shape[2]), BF16),
        ]
        + (
            [pltpu.VMEM(field.shape, BF16), pltpu.SemaphoreType.DMA((len(mix_chunks(channels)),))]
            if last
            else []
        ),
        compiler_params=pltpu.CompilerParams(vmem_limit_bytes=14 << 20),
        cost_estimate=pl.CostEstimate(
            flops=5 << 30, bytes_accessed=8 << 20, transcendentals=1 << 20
        ),
        name="finish",
    )(band, far_edge, far_body, far_halo, *parts, mixes, field, first, second)


def shards(grid_state, filter_taps, support_start, support_count, filter_mix, w_in, w_out):
    reach = grid_state.shape[1]
    layers = w_in.shape[0]
    polar, ring = lax.axis_size("polar"), lax.axis_size("azimuth")
    near_route = [(i, i ^ 1) for i in range(ring)]
    far_route = [(i, (i + 1 if i % 2 else i - 1) % ring) for i in range(ring)]
    down_route = [(i, (i + 1) % polar) for i in range(polar)]
    up_route = [(i, (i - 1) % polar) for i in range(polar)]
    here = lax.axis_index("polar")
    parity = lax.rem(lax.axis_index("azimuth"), 2).reshape(1)
    info = jnp.concatenate([support_start, support_count, parity])

    def halo_of(above, below):
        above = jnp.where(here > 0, above, jnp.zeros_like(above))
        below = jnp.where(here < polar - 1, below, jnp.zeros_like(below))
        return jnp.concatenate([above, below], axis=0)

    mixes = jnp.transpose(filter_mix, (1, 0, 2))
    field = grid_state
    down, up, edge, body = fetch(field)
    for layer in range(layers):
        far_edge = lax.ppermute(edge, "azimuth", far_route)
        far_body = lax.ppermute(body, "azimuth", far_route)
        near = lax.ppermute(field, "azimuth", near_route)
        above = lax.ppermute(down, "polar", down_route)
        below = lax.ppermute(up, "polar", up_route)
        if layer == 0:
            band = make_bands(info, filter_taps, reach)
        inner = conv_local(layer, info, band, field, near, mixes)
        far_above = lax.ppermute(far_edge[:2], "polar", down_route)
        far_below = lax.ppermute(far_edge[2:], "polar", up_route)
        halo = halo_of(above, below)
        near_halo = lax.ppermute(halo, "azimuth", near_route)
        outer = conv_local(layer, info, band, field, near, mixes, (halo, near_halo))
        out = finish(
            layer, layer == layers - 1, band, far_edge, far_body,
            halo_of(far_above, far_below), (inner, outer), mixes, field, w_in, w_out,
        )
        field, (down, up, edge, body) = out[0], out[1:] or (None,) * 4
    return field


def solution(mesh):
    return jax.shard_map(
        shards,
        mesh=mesh,
        in_specs=(
            P("polar", "azimuth", None),
            P("polar", None, None, None),
            P("polar"),
            P("polar"),
            P(),
            P(),
            P(),
        ),
        out_specs=P("polar", "azimuth", None),
        check_vma=False,
    )
```
